256 devices in a mesh: ctx: 64 (over x, z, y_lo), exp: 4 (over y_hi, core).
Axes of the slice: x: 4, y: 4 (y_hi: 2, y_lo: 2; y = y_hi * 2 + y_lo), z: 8, core: 2. Of those that a mesh axis runs over, the one named last changes fastest.
Arguments:
- query_rows: bfloat16 [32768, 3072], P(('ctx', 'exp')), may hold values from -6 to 6
- key_rows: bfloat16 [32768, 512], P('ctx'), may hold values from -6 to 6
- value_matrix: bfloat16 [32768, 512], P('ctx'), may hold values from -6 to 6
- out_grads: bfloat16 [32768, 3072], P(('ctx', 'exp')), may hold values from -6 to 6
- doc_start: int32 [32768], P(('ctx', 'exp')), may hold values from 0 to 32767, as said below
- moe_grads: bfloat16 [32768, 6144], P(('ctx', 'exp')), may hold values from -6 to 6
- expert_out: bfloat16 [32768, 2, 6144], P(('ctx', 'exp')), may hold values from -0.079589844 to 0.079589844
- gate_logits: float32 [32768, 2], P(('ctx', 'exp')), may hold values from -8 to 8
- routes: int32 [32768, 2], P(('ctx', 'exp')), may hold values from 0 to 7, all different within a row; in each aligned block of 128 rows (0 to 127, 128 to 255, ...) at most 40 rows name the same one
Outputs:
- query_grads: bfloat16 [32768, 3072], P(('ctx', 'exp'))
- key_grads: bfloat16 [32768, 512], P('ctx', 'exp')
- value_grads: bfloat16 [32768, 512], P('ctx', 'exp')
- expert_grads: bfloat16 [64, 8, 4, 40, 6144], P('ctx', 'exp')
- logit_grads: float32 [32768, 2], P(('ctx', 'exp'))
The draws below stay inside these ranges and needn't reach their ends.
Inputs may be any that keep to these rules, and one draw needn't show every extreme that they name: doc_start[t] is the first position of the document that holds position t: at most t, never falling along the sequence, equal to t where a document begins; position 0 begins one, and so does the last position. `routes`: each token names two different experts; within each aligned block of 128 tokens (the tokens of one device) no expert is named by more than 40 tokens, a bound that some block reaches.
All inputs are finite; a program needn't handle non-finite values.
Results may differ from the reference program's by a relative error of at most 0.02.
Values may be sent and summed in bfloat16 or wider, within the bound.
No kernel may reach another device: no remote copies, remote signals or barrier semaphores. Data moves between devices by JAX's collectives and lax.ppermute only.
A program may use at most 192 MiB of HBM per device.

```python
import math
import jax
import jax.numpy as jnp
import numpy as np
from jax import lax

D = 6144
QUERY_HEADS = 24
KEY_VALUE_HEADS = 4
HEAD_SIZE = 128
EXPERTS = 8
TOK_DEV = 128
TC = 512
SEQUENCE_TOKENS = 32768
CAP = 40
N_CTX = 64
N_EXP = 4


def paired_rows(key):
    query_vals = jnp.clip(jax.random.normal(jax.random.fold_in(key, 11), (SEQUENCE_TOKENS, QUERY_HEADS * HEAD_SIZE), jnp.float32), -6.0, 6.0)
    key_entries = jnp.clip(jax.random.normal(jax.random.fold_in(key, 12), (SEQUENCE_TOKENS, KEY_VALUE_HEADS * HEAD_SIZE), jnp.float32), -6.0, 6.0)
    return (query_vals, key_entries)


def draw_query_rows(key, part):
    return paired_rows(key)[0].astype(jnp.bfloat16)


def draw_key_rows(key, part):
    return paired_rows(key)[1].astype(jnp.bfloat16)


def draw_doc_start(key, part):
    token_position = jnp.arange(SEQUENCE_TOKENS, dtype=jnp.int32)
    marks = jax.random.randint(jax.random.fold_in(key, 21), (SEQUENCE_TOKENS,), 0, 2 * TC) == 0
    marks = marks | (token_position == 0) | (token_position == SEQUENCE_TOKENS - 1)
    starts = lax.cummax(jnp.where(marks, token_position, 0), axis=0)
    return starts.astype(jnp.int32)


def level_of(rng, extent, cuts, low, top_value):
    def one(position, parts):
        steps = jax.random.uniform(jax.random.fold_in(jax.random.fold_in(rng, 6), position), (parts,), jnp.float32, low / len(cuts), top_value / len(cuts))
        return jnp.repeat(jnp.exp(steps), extent[position] // parts).reshape((-1,) + (1,) * (len(extent) - position - 1))

    level = one(*cuts[0])
    for cut in cuts[1:]:
        level = level * one(*cut)
    return level


def assign_block(rng, own, number, rows, count, top, most, skew):
    ranking = jax.random.permutation(rng, count)
    crowded, ordinary = load_shares(count, rows * top, most, skew, True), load_shares(count, rows * top, most, skew, False)
    places = jnp.arange(count)

    def named(lengths, rotation):
        used = int((lengths > 0).sum())
        fixed = max(1, used // 4)
        moved = fixed + (places - fixed + rotation * (used - fixed)) % max(1, count - fixed)
        return jnp.zeros((count,), jnp.int32).at[ranking[jnp.where(places < fixed, places, moved)]].set(jnp.asarray(lengths, jnp.int32))

    lengths = jnp.where(number % 4 == 0, named(crowded, number // 4), named(ordinary, number - number // 4 - 1))
    mixed = jax.random.permutation(jax.random.fold_in(own, 3), count)
    source_of, taker = mixed[0:count // 2 * 2:2], mixed[1:count // 2 * 2:2]
    room = jnp.minimum(lengths[source_of] - 1, most - lengths[taker]) // 2
    room = jnp.where((source_of == ranking[0]) | (taker == ranking[0]) | (lengths[taker] == 0), 0, jnp.maximum(room, 0))
    moved = jax.random.randint(jax.random.fold_in(own, 4), (count // 2,), 0, 1 << 20) % (room + 1)
    lengths = lengths.at[source_of].add(-moved).at[taker].add(moved)
    members = jnp.searchsorted(jnp.cumsum(lengths), jnp.arange(rows * top), side="right").astype(jnp.int32)
    table = members.reshape(top, rows).T
    table = table[jax.random.permutation(jax.random.fold_in(own, 1), rows)]
    rotation = jax.random.randint(jax.random.fold_in(own, 2), (rows, 1), 0, top)
    return jnp.take_along_axis(table, (jnp.arange(top)[None, :] + rotation) % top, axis=1)


def load_shares(amount, total, reach, slope, full):
    weights = [(1 << 20) // math.isqrt(standing ** slope) + 1 for standing in range(1, amount + 1)]
    largest = reach if full else min(reach, max(-(-total // amount), total * weights[0] // sum(weights)))
    least = 1 if total - largest >= amount - 1 else 0
    holding, rest = [largest] + [least] * (amount - 1), total - largest - least * (amount - 1)
    while rest > 0:
        movable = [i for i in range(1, amount) if holding[i] < largest] or [i for i in range(1, amount) if holding[i] < reach]
        mass, budget = sum([weights[i] for i in movable]), rest
        for i in movable:
            extra = min(reach - holding[i], max(1, budget * weights[i] // mass), rest)
            holding[i] = holding[i] + extra
            rest = rest - extra
    return np.array(holding)


def scatter_about(key, shape, scale, limit, shards=(), kind=jnp.bfloat16):
    entries = jax.random.normal(key, shape, jnp.float32) * scale
    if len(shards) > 0:
        entries = level_of(key, shape, shards, -0.22, 0.18) * entries
    return jnp.clip(entries, min=-limit, max=limit).astype(kind)


def setup_inputs(seed: int = 0) -> dict:
    seeds = jax.random.split(jax.random.key(seed), 10)
    query_rows = draw_query_rows(jax.random.fold_in(seeds[9], 71), 0)
    key_rows = draw_key_rows(jax.random.fold_in(seeds[9], 71), 0)
    value_matrix = scatter_about(seeds[2], (SEQUENCE_TOKENS, KEY_VALUE_HEADS * HEAD_SIZE), 1.0, 6.0, ((0, 64),))
    out_grads = scatter_about(seeds[3], (SEQUENCE_TOKENS, QUERY_HEADS * HEAD_SIZE), 1.0, 6.0, ((0, 256),))
    doc_start = draw_doc_start(jax.random.fold_in(seeds[9], 71), 0)
    moe_grads = scatter_about(seeds[5], (SEQUENCE_TOKENS, D), 1.0, 6.0, ((0, 256),))
    expert_out = scatter_about(seeds[6], (SEQUENCE_TOKENS, 2, D), 0.0128, 0.079589844, ((0, 256),))
    gate_logits = scatter_about(seeds[7], (SEQUENCE_TOKENS, 2), 2.0, 8.0, ((0, 256),), jnp.float32)
    routes_keys = jax.random.split(jax.random.fold_in(seeds[8], 1), SEQUENCE_TOKENS // TOK_DEV)
    routes_turns = jax.random.permutation(jax.random.fold_in(seeds[8], 3), SEQUENCE_TOKENS // TOK_DEV)
    routes = jax.vmap(lambda own, number: assign_block(jax.random.fold_in(seeds[8], 2), own, number, TOK_DEV, EXPERTS, 2, CAP, 2))(routes_keys, routes_turns).reshape((SEQUENCE_TOKENS, 2))
    return dict(query_rows=query_rows, key_rows=key_rows, value_matrix=value_matrix, out_grads=out_grads, doc_start=doc_start, moe_grads=moe_grads, expert_out=expert_out, gate_logits=gate_logits, routes=routes)


def attend(query_block, grad_block, key_block, value_block, allowed):
    heads = query_block.shape[1] // HEAD_SIZE
    groups = key_block.shape[1] // HEAD_SIZE
    share = heads // groups
    count_rows = query_block.shape[0]
    count_keys = key_block.shape[0]
    factor = 1.0 / math.sqrt(HEAD_SIZE)
    queries = query_block.astype(jnp.float32).reshape(count_rows, groups, share, HEAD_SIZE)
    grads = grad_block.astype(jnp.float32).reshape(count_rows, groups, share, HEAD_SIZE)
    key_f = key_block.astype(jnp.float32).reshape(count_keys, groups, HEAD_SIZE)
    value_f = value_block.astype(jnp.float32).reshape(count_keys, groups, HEAD_SIZE)
    scores = jnp.einsum('rgjd,sgd->gjrs', queries, key_f) * factor
    scores = jnp.where(allowed[None, None], scores, -jnp.inf)
    peak = lax.optimization_barrier(jnp.max(scores, axis=-1, keepdims=True))
    weights = jnp.exp(scores - peak)
    probs = weights / lax.optimization_barrier(jnp.sum(weights, axis=-1, keepdims=True))
    probs_low = lax.optimization_barrier(probs.astype(jnp.bfloat16)).astype(jnp.float32)
    output = jnp.einsum('gjrs,sgd->rgjd', probs_low, value_f)
    delta = jnp.einsum('rgjd,rgjd->gjr', grads, output)
    dprobs = jnp.einsum('rgjd,sgd->gjrs', grads, value_f)
    dscores = probs * (dprobs - delta[..., None])
    dscores_low = lax.optimization_barrier(dscores.astype(jnp.bfloat16)).astype(jnp.float32)
    query_grad = (jnp.einsum('gjrs,sgd->rgjd', dscores_low, key_f) * factor).reshape(count_rows, heads * HEAD_SIZE)
    key_grad = (jnp.einsum('gjrs,rgjd->sgd', dscores_low, queries) * factor).reshape(count_keys, groups * HEAD_SIZE)
    value_grad = jnp.einsum('gjrs,rgjd->sgd', probs_low, grads).reshape(count_keys, groups * HEAD_SIZE)
    return (query_grad.astype(jnp.bfloat16), key_grad, value_grad)

def slot_numbers(flat_routes):
    onehot = (flat_routes[..., None] == jnp.arange(EXPERTS, dtype=jnp.int32)).astype(jnp.int32)
    before = jnp.cumsum(onehot, axis=-2) - onehot
    return lax.optimization_barrier(jnp.sum(before * onehot, axis=-1)).astype(jnp.int32)

def reference(query_rows, key_rows, value_matrix, out_grads, doc_start, moe_grads, expert_out, gate_logits, routes):
    column_range = KEY_VALUE_HEADS * HEAD_SIZE
    key_pad = jnp.concatenate([jnp.zeros((TC, column_range), key_rows.dtype), key_rows], axis=0)
    value_pad = jnp.concatenate([jnp.zeros((TC, column_range), value_matrix.dtype), value_matrix], axis=0)

    def attn_step(carry, block):
        key_acc, value_acc = carry
        first = (block * TC).astype(jnp.int32)
        query_block = lax.dynamic_slice_in_dim(query_rows, first, TC, 0)
        grad_block = lax.dynamic_slice_in_dim(out_grads, first, TC, 0)
        start_block = lax.dynamic_slice_in_dim(doc_start, first, TC, 0)
        key_block = lax.dynamic_slice_in_dim(key_pad, first, 2 * TC, 0)
        value_block = lax.dynamic_slice_in_dim(value_pad, first, 2 * TC, 0)
        query_pos = first + jnp.arange(TC, dtype=jnp.int32)
        key_pos = first - TC + jnp.arange(2 * TC, dtype=jnp.int32)
        allowed = (key_pos[None, :] >= start_block[:, None]) & (key_pos[None, :] <= query_pos[:, None])
        query_grad, key_part, value_part = attend(query_block, grad_block, key_block, value_block, allowed)
        key_acc = lax.dynamic_update_slice_in_dim(key_acc, lax.dynamic_slice_in_dim(key_acc, first, 2 * TC, 0) + key_part, first, 0)
        value_acc = lax.dynamic_update_slice_in_dim(value_acc, lax.dynamic_slice_in_dim(value_acc, first, 2 * TC, 0) + value_part, first, 0)
        return ((key_acc, value_acc), query_grad)
    zeros_acc = jnp.zeros((SEQUENCE_TOKENS + TC, column_range), jnp.float32)
    (key_acc, value_acc), query_blocks = lax.scan(attn_step, (zeros_acc, zeros_acc), jnp.arange(N_CTX, dtype=jnp.int32))
    query_grads = query_blocks.reshape(SEQUENCE_TOKENS, QUERY_HEADS * HEAD_SIZE)
    key_grads = key_acc[TC:].astype(jnp.bfloat16)
    value_grads = value_acc[TC:].astype(jnp.bfloat16)

    def moe_step(block):
        first = (block * TC).astype(jnp.int32)
        grad_rows = lax.dynamic_slice_in_dim(moe_grads, first, TC, 0)
        saved = lax.dynamic_slice_in_dim(expert_out, first, TC, 0)
        logits = lax.dynamic_slice_in_dim(gate_logits, first, TC, 0)
        chosen = lax.dynamic_slice_in_dim(routes, first, TC, 0)
        gate = jax.nn.sigmoid(logits - logits[:, ::-1])
        scaled = (gate[:, :, None] * grad_rows.astype(jnp.float32)[:, None, :]).astype(jnp.bfloat16).reshape(TC * 2, D)
        flat_routes = chosen.reshape(N_EXP, 2 * TOK_DEV)
        slots = slot_numbers(flat_routes)
        source = jnp.arange(N_EXP, dtype=jnp.int32)[:, None]
        token_position = ((flat_routes * N_EXP + source) * CAP + slots).reshape(-1)
        buffer = jnp.zeros((EXPERTS * N_EXP * CAP, D), jnp.bfloat16).at[token_position].set(scaled)
        gate_grad = jnp.einsum('td,tad->ta', grad_rows.astype(jnp.float32), saved.astype(jnp.float32))
        logit_part = gate * (gate_grad - lax.optimization_barrier(jnp.sum(gate * gate_grad, axis=-1, keepdims=True)))
        return (buffer.reshape(EXPERTS, N_EXP, CAP, D), logit_part)
    expert_grads, logit_blocks = lax.map(moe_step, jnp.arange(N_CTX, dtype=jnp.int32))
    logit_grads = logit_blocks.reshape(SEQUENCE_TOKENS, 2)
    return (query_grads, key_grads, value_grads, expert_grads, logit_grads)
```

```python
import functools
import math

import jax
import jax.numpy as jnp
from jax import lax
from jax.experimental import pallas as pl
from jax.experimental.pallas import tpu as pltpu
from jax.sharding import PartitionSpec as P

HEAD_SIZE = 128
EXPERTS = 8
CAP = 40
AXES = ("ctx", "exp")
BLOCK = 512
SHARE = 6
CHUNK = 256
FACTOR = 1.0 / math.sqrt(HEAD_SIZE)
LOG2E = math.log2(math.e)
NEG = -1e30


def routes_of(fn):
    blocks, group = lax.axis_size("ctx"), lax.axis_size("exp")
    pairs = []
    for b in range(blocks):
        for e in range(group):
            tb, te = fn(b, e)
            pairs.append((b * group + e, (tb % blocks) * group + te))
    return pairs


def send(x, fn):
    return lax.ppermute(x, AXES, routes_of(fn))


def to_core(b, e):
    return b, e ^ 1


def to_cross(b, e):
    return b, e ^ 2


def to_next_same(b, e):
    return b + 1, e


def to_next_other(b, e):
    return b + 1, e ^ 2


def to_prev_same(b, e):
    return b - 1, e


def to_prev_other(b, e):
    return b - 1, e ^ 2


def pack_kv_kernel(s_ref, k_ref, v_ref, ko_ref, vo_ref):
    ko_ref[...] = k_ref[...]
    vo_ref[...] = v_ref[...]


def pack_kv(scal, keys, values):
    rows = keys.shape[0]
    pick = lambda g, s: (0, 2 * g + s[0])
    spec = pl.BlockSpec((rows, HEAD_SIZE), pick)
    out = pl.BlockSpec((rows, HEAD_SIZE), lambda g, s: (0, g))
    shape = jax.ShapeDtypeStruct((rows, 2 * HEAD_SIZE), keys.dtype)
    return pl.pallas_call(
        pack_kv_kernel,
        grid_spec=pltpu.PrefetchScalarGridSpec(
            num_scalar_prefetch=1, grid=(2,), in_specs=[spec, spec], out_specs=[out, out]
        ),
        out_shape=[shape, shape],
        name="pack_kv",
    )(scal, keys, values)


def pack_qg_kernel(s_ref, q_ref, g_ref, logit_ref, route_ref, doc_ref, out_ref, meta_ref):
    wide = q_ref.shape[1]
    out_ref[0, :, :wide] = q_ref[...]
    out_ref[0, :, wide:] = g_ref[...]

    @pl.when(pl.program_id(0) == 0)
    def _():
        tokens = logit_ref.shape[1]
        logits = logit_ref[...]
        routes = route_ref[...]
        l0, l1 = logits[0:1], logits[1:2]
        r0, r1 = routes[0:1], routes[1:2]
        gate0 = jax.nn.sigmoid(l0 - l1)
        gate1 = jax.nn.sigmoid(l1 - l0)
        expert = lax.broadcasted_iota(jnp.int32, (EXPERTS, tokens), 0)
        hit0 = (jnp.broadcast_to(r0, (EXPERTS, tokens)) == expert).astype(jnp.float32)
        hit1 = (jnp.broadcast_to(r1, (EXPERTS, tokens)) == expert).astype(jnp.float32)
        hits = hit0 + hit1
        earlier = (
            lax.broadcasted_iota(jnp.int32, (tokens, tokens), 0)
            < lax.broadcasted_iota(jnp.int32, (tokens, tokens), 1)
        ).astype(jnp.float32)
        before = jnp.dot(hits, earlier, preferred_element_type=jnp.float32)
        slot0 = jnp.sum(before * hit0, axis=0, keepdims=True)
        slot1 = jnp.sum(before * hit1, axis=0, keepdims=True)
        meta_ref[0:1] = r0.astype(jnp.float32) * CAP + slot0
        meta_ref[1:2] = r1.astype(jnp.float32) * CAP + slot1
        meta_ref[2:3] = gate0
        meta_ref[3:4] = gate1
        meta_ref[4:5] = doc_ref[...].astype(jnp.float32)
        meta_ref[5:8] = jnp.zeros((3, tokens), jnp.float32)


def pack_qg(scal, queries, grads, logits_t, routes_t, doc_row):
    rows, width = queries.shape
    wide = SHARE * HEAD_SIZE
    pick = lambda g, s: (0, 2 * g + 1 - s[0])
    whole = lambda a: pl.BlockSpec(a.shape, lambda g, s: (0, 0))
    return pl.pallas_call(
        pack_qg_kernel,
        grid_spec=pltpu.PrefetchScalarGridSpec(
            num_scalar_prefetch=1,
            grid=(2,),
            in_specs=[
                pl.BlockSpec((rows, wide), pick),
                pl.BlockSpec((rows, wide), pick),
                whole(logits_t),
                whole(routes_t),
                whole(doc_row),
            ],
            out_specs=[
                pl.BlockSpec((1, rows, 2 * wide), lambda g, s: (g, 0, 0)),
                pl.BlockSpec((8, rows), lambda g, s: (0, 0)),
            ],
        ),
        out_shape=[
            jax.ShapeDtypeStruct((2, rows, 2 * wide), queries.dtype),
            jax.ShapeDtypeStruct((8, rows), jnp.float32),
        ],
        name="pack_qg",
    )(scal, queries, grads, logits_t, routes_t, doc_row)


def nt(a, b):
    return lax.dot_general(a, b, (((1,), (1,)), ((), ())), preferred_element_type=jnp.float32)


def attend_kernel(
    heads_per_step,
    s_ref,
    q_ref,
    g_ref,
    qp_ref,
    gp_ref,
    kp_ref,
    ko_ref,
    vp_ref,
    vo_ref,
    meta_ref,
    metap_ref,
    dqo_ref,
    dqp_ref,
    prev_ref,
    own_ref,
    bias,
    kt,
    score,
    grad,
    low,
    dk,
    dv,
):
    step = pl.program_id(0)
    rows = q_ref.shape[0]
    tokens = 2 * rows
    span = kp_ref.shape[0]
    half = span // CHUNK

    def keys(c):
        return kp_ref[pl.ds(c * CHUNK, CHUNK), :] if c < half else ko_ref[pl.ds((c - half) * CHUNK, CHUNK), :]

    def values(c):
        return vp_ref[pl.ds(c * CHUNK, CHUNK), :] if c < half else vo_ref[pl.ds((c - half) * CHUNK, CHUNK), :]

    @pl.when(step == 0)
    def _():
        core, side, ctx = s_ref[0], s_ref[1], s_ref[2]
        base = (ctx - 1) * span
        mine = ctx * span + (2 * side + core) * rows
        theirs = ctx * span + (2 * side + 1 - core) * rows
        lane = lax.broadcasted_iota(jnp.int32, (1, rows), 1)
        qpos = jnp.concatenate([mine + lane, theirs + lane], axis=1)
        doc = jnp.concatenate([meta_ref[4:5], metap_ref[4:5]], axis=1).astype(jnp.int32)
        for c in range(2 * half):
            kpos = base + c * CHUNK + lax.broadcasted_iota(jnp.int32, (CHUNK, tokens), 0)
            ok = (kpos >= doc) & (kpos <= qpos)
            bias[pl.ds(c * CHUNK, CHUNK), :] = jnp.where(ok, 0.0, NEG)
            kt[:, pl.ds(c * CHUNK, CHUNK)] = keys(c).T
        dk[...] = jnp.zeros_like(dk)
        dv[...] = jnp.zeros_like(dv)

    for h in range(heads_per_step):
        cols = slice(h * HEAD_SIZE, (h + 1) * HEAD_SIZE)
        q2 = jnp.concatenate([q_ref[:, cols], qp_ref[0, :, cols]], axis=0)
        g2 = jnp.concatenate([g_ref[:, cols], gp_ref[0, :, cols]], axis=0)
        peak = None
        for c in range(2 * half):
            at = pl.ds(c * CHUNK, CHUNK)
            s = nt(keys(c), q2) * (FACTOR * LOG2E) + bias[at, :]
            score[h, at, :] = s
            top = jnp.max(s, axis=0, keepdims=True)
            peak = top if peak is None else jnp.maximum(peak, top)
        total = None
        for c in range(2 * half):
            at = pl.ds(c * CHUNK, CHUNK)
            w = jnp.exp2(score[h, at, :] - peak)
            score[h, at, :] = w
            part = jnp.sum(w, axis=0, keepdims=True)
            total = part if total is None else total + part
        inv = 1.0 / total
        delta = None
        for c in range(2 * half):
            at = pl.ds(c * CHUNK, CHUNK)
            p = score[h, at, :] * inv
            score[h, at, :] = p
            pl_low = p.astype(jnp.bfloat16)
            low[h, at, :] = pl_low
            dp = nt(values(c), g2)
            grad[h, at, :] = dp
            part = jnp.sum(pl_low.astype(jnp.float32) * dp, axis=0, keepdims=True)
            delta = part if delta is None else delta + part
        dqt = None
        for c in range(2 * half):
            at = pl.ds(c * CHUNK, CHUNK)
            ds = (score[h, at, :] * (grad[h, at, :] - delta)).astype(jnp.bfloat16)
            dk[at, :] += jnp.dot(ds, q2, preferred_element_type=jnp.float32)
            dv[at, :] += jnp.dot(low[h, at, :], g2, preferred_element_type=jnp.float32)
            part = jnp.dot(kt[:, at], ds, preferred_element_type=jnp.float32)
            dqt = part if dqt is None else dqt + part
        dq = (dqt * FACTOR).T.astype(jnp.bfloat16)
        dqo_ref[:, cols] = dq[:rows]
        dqp_ref[:, cols] = dq[rows:]

    @pl.when(step == pl.num_programs(0) - 1)
    def _():
        prev_ref[:, :HEAD_SIZE] = (dk[:span, :] * FACTOR).astype(prev_ref.dtype)
        prev_ref[:, HEAD_SIZE:] = dv[:span, :].astype(prev_ref.dtype)
        own_ref[:, :HEAD_SIZE] = (dk[span:, :] * FACTOR).astype(own_ref.dtype)
        own_ref[:, HEAD_SIZE:] = dv[span:, :].astype(own_ref.dtype)


def attend(scal, queries, grads, payload, keys_prev, keys, values_prev, values, meta, meta_core, which, own_dtype, name):
    heads_per_step = 2
    steps = SHARE // heads_per_step
    rows = queries.shape[0]
    span = keys.shape[0]
    wide = heads_per_step * HEAD_SIZE
    qcol = lambda j, s: (0, steps * (2 * s[3] + s[0]) + j)
    kcol = lambda j, s: (0, 2 * s[3] + s[0])
    pcol = lambda j, s: (0, s[3])
    zero = lambda j, s: (0, 0)
    return pl.pallas_call(
        functools.partial(attend_kernel, heads_per_step),
        grid_spec=pltpu.PrefetchScalarGridSpec(
            num_scalar_prefetch=1,
            grid=(steps,),
            in_specs=[
                pl.BlockSpec((rows, wide), qcol),
                pl.BlockSpec((rows, wide), qcol),
                pl.BlockSpec((1, rows, wide), lambda j, s: (s[3], 0, j)),
                pl.BlockSpec((1, rows, wide), lambda j, s: (s[3], 0, steps + j)),
                pl.BlockSpec((span, HEAD_SIZE), pcol),
                pl.BlockSpec((span, HEAD_SIZE), kcol),
                pl.BlockSpec((span, HEAD_SIZE), pcol),
                pl.BlockSpec((span, HEAD_SIZE), kcol),
                pl.BlockSpec((8, rows), zero),
                pl.BlockSpec((8, rows), zero),
            ],
            out_specs=[
                pl.BlockSpec((rows, wide), lambda j, s: (0, j)),
                pl.BlockSpec((rows, wide), lambda j, s: (0, j)),
                pl.BlockSpec((span, 2 * HEAD_SIZE), zero),
                pl.BlockSpec((span, 2 * HEAD_SIZE), zero),
            ],
            scratch_shapes=[
                pltpu.VMEM((2 * span, 2 * rows), jnp.float32),
                pltpu.VMEM((HEAD_SIZE, 2 * span), jnp.bfloat16),
                pltpu.VMEM((heads_per_step, 2 * span, 2 * rows), jnp.float32),
                pltpu.VMEM((heads_per_step, 2 * span, 2 * rows), jnp.float32),
                pltpu.VMEM((heads_per_step, 2 * span, 2 * rows), jnp.bfloat16),
                pltpu.VMEM((2 * span, HEAD_SIZE), jnp.float32),
                pltpu.VMEM((2 * span, HEAD_SIZE), jnp.float32),
            ],
        ),
        out_shape=[
            jax.ShapeDtypeStruct((rows, SHARE * HEAD_SIZE), jnp.bfloat16),
            jax.ShapeDtypeStruct((rows, SHARE * HEAD_SIZE), jnp.bfloat16),
            jax.ShapeDtypeStruct((span, 2 * HEAD_SIZE), jnp.bfloat16),
            jax.ShapeDtypeStruct((span, 2 * HEAD_SIZE), own_dtype),
        ],
        cost_estimate=pl.CostEstimate(flops=2_400_000_000, bytes_accessed=4_000_000, transcendentals=1_500_000),
        name=name,
    )(jnp.concatenate([scal[:3], which.reshape(1)]), queries, grads, payload, payload, keys_prev, keys, values_prev, values, meta, meta_core)


def place_kernel(s_ref, rows_a, rows_b, meta_a, meta_b, *rest):
    out_ref = rest[-1]
    tokens = rows_a.shape[0]
    local = out_ref.shape[1]

    def emit(rows_ref, meta_ref):
        first = s_ref[2] * (local * CAP)
        slot = (first + lax.broadcasted_iota(jnp.int32, (local * CAP, tokens), 0)).astype(jnp.float32)
        hit0 = slot == meta_ref[0:1]
        hit1 = slot == meta_ref[1:2]
        gate = jnp.sum(
            jnp.where(hit0, meta_ref[2:3], 0.0) + jnp.where(hit1, meta_ref[3:4], 0.0),
            axis=1,
            keepdims=True,
        )
        onehot = (hit0 | hit1).astype(jnp.float32).astype(jnp.bfloat16)
        picked = jnp.dot(onehot, rows_ref[...], preferred_element_type=jnp.float32)
        scaled = (picked * gate).astype(out_ref.dtype)
        for k in range(local):
            out_ref[0, k, 0] = scaled[k * CAP : (k + 1) * CAP]

    step = pl.program_id(0)

    @pl.when(step == 0)
    def _():
        emit(rows_a, meta_a)

    @pl.when(step == 1)
    def _():
        emit(rows_b, meta_b)


def place(scal, rows_a, rows_b, meta_a, meta_b, group, into, name):
    tokens, width = rows_a.shape
    local = EXPERTS // group
    zero = lambda i, s: (0, 0)
    ins = [
        pl.BlockSpec((tokens, width), zero),
        pl.BlockSpec((tokens, width), zero),
        pl.BlockSpec((8, tokens), zero),
        pl.BlockSpec((8, tokens), zero),
    ]
    args = [rows_a, rows_b, meta_a, meta_b]
    alias = {}
    if into is not None:
        ins.append(pl.BlockSpec(memory_space=pl.ANY))
        args.append(into)
        alias = {5: 0}
    return pl.pallas_call(
        place_kernel,
        grid_spec=pltpu.PrefetchScalarGridSpec(
            num_scalar_prefetch=1,
            grid=(2,),
            in_specs=ins,
            out_specs=pl.BlockSpec((1, local, 1, CAP, width), lambda i, s: (0, 0, s[i], 0, 0)),
        ),
        out_shape=jax.ShapeDtypeStruct((1, local, group, CAP, width), rows_a.dtype),
        input_output_aliases=alias,
        cost_estimate=pl.CostEstimate(flops=500_000_000, bytes_accessed=5_200_000, transcendentals=0),
        name=name,
    )(scal, *args)


def finish_kernel(s_ref, own_ref, cross_ref, same_ref, other_ref, near, far, near_part, far_part, k_ref, v_ref, dq_ref):
    total = (
        own_ref[...]
        + cross_ref[...].astype(jnp.float32)
        + same_ref[...].astype(jnp.float32)
        + other_ref[...].astype(jnp.float32)
    ).astype(k_ref.dtype)
    k_ref[...] = total[:, :HEAD_SIZE]
    v_ref[...] = total[:, HEAD_SIZE:]
    wide = SHARE * HEAD_SIZE

    for core in range(2):
        for side in range(2):

            @pl.when((s_ref[0] == core) & (s_ref[1] == side))
            def _():
                for position, mine, part in ((side, near, near_part), (1 - side, far, far_part)):
                    at = 2 * position + core
                    dq_ref[:, at * wide : (at + 1) * wide] = mine[...]
                    at = 2 * position + 1 - core
                    dq_ref[:, at * wide : (at + 1) * wide] = part[...]


def finish(scal, own, cross, same, other, mine0, mine1, part0, part1):
    span = own.shape[0]
    rows, wide = mine0.shape
    zero = lambda i, s: (0, 0)
    args = [own, cross, same, other, mine0, mine1, part0, part1]
    return pl.pallas_call(
        finish_kernel,
        grid_spec=pltpu.PrefetchScalarGridSpec(
            num_scalar_prefetch=1,
            grid=(1,),
            in_specs=[pl.BlockSpec(a.shape, zero) for a in args],
            out_specs=[
                pl.BlockSpec((span, HEAD_SIZE), zero),
                pl.BlockSpec((span, HEAD_SIZE), zero),
                pl.BlockSpec((rows, 4 * wide), zero),
            ],
        ),
        out_shape=[
            jax.ShapeDtypeStruct((span, HEAD_SIZE), jnp.bfloat16),
            jax.ShapeDtypeStruct((span, HEAD_SIZE), jnp.bfloat16),
            jax.ShapeDtypeStruct((rows, 4 * wide), jnp.bfloat16),
        ],
        name="finish",
    )(scal, *args)


def local(
    query_rows,
    key_rows,
    value_matrix,
    out_grads,
    doc_start,
    moe_grads,
    expert_out,
    gate_logits,
    routes,
):
    rows = query_rows.shape[0]
    group = lax.axis_size("exp")
    ctx_pos = lax.axis_index("ctx").astype(jnp.int32)
    exp_pos = lax.axis_index("exp").astype(jnp.int32)
    core = exp_pos % 2
    side = exp_pos // 2
    scal = jnp.stack([core, side, ctx_pos])

    kpay, vpay = pack_kv(scal, key_rows, value_matrix)
    keys_prev = send(kpay, to_next_same)
    values_prev = send(vpay, to_next_other)
    payload, meta = pack_qg(
        scal, query_rows, out_grads, gate_logits.T, routes.T, doc_start.reshape(1, rows)
    )
    payload = send(payload, to_core)
    meta_core = send(meta, to_core)
    meta_cross = send(meta, to_cross)
    meta_diag = send(meta_cross, to_core)
    rows_cross = send(moe_grads, to_cross)
    rows_core = send(moe_grads, to_core)
    rows_diag = send(rows_cross, to_core)

    gate = jax.nn.sigmoid(gate_logits - gate_logits[:, ::-1])
    gate_grad = jnp.einsum("td,tad->ta", moe_grads, expert_out, preferred_element_type=jnp.float32)
    logit_grads = gate * (gate_grad - jnp.sum(gate * gate_grad, axis=-1, keepdims=True))

    near = place(
        jnp.stack([exp_pos, exp_pos ^ 1, exp_pos]), moe_grads, rows_core, meta, meta_core, group, None, "place_near"
    )
    both = functools.partial(
        attend, scal, query_rows, out_grads, payload, keys_prev, key_rows, values_prev, value_matrix, meta, meta_core
    )
    dqo_far, dqp_far, prev_far, own_far = both(1 - side, jnp.bfloat16, "attend_far")
    cross = send(own_far, to_cross)
    back_other = send(prev_far, to_prev_other)
    part_far = send(dqp_far, to_core)
    dqo_near, dqp_near, prev_near, own_near = both(side, jnp.float32, "attend_near")
    back_same = send(prev_near, to_prev_same)
    part_near = send(dqp_near, to_core)

    expert_grads = place(
        jnp.stack([exp_pos ^ 2, exp_pos ^ 3, exp_pos]), rows_cross, rows_diag, meta_cross, meta_diag, group, near, "place_far"
    )
    key_grads, value_grads, query_grads = finish(
        jnp.stack([core, side]), own_near, cross, back_same, back_other, dqo_near, dqo_far, part_near, part_far
    )
    return (query_grads, key_grads, value_grads, expert_grads, logit_grads)


def solution(mesh):
    in_specs = (
        P(("ctx", "exp"), None),
        P("ctx", None),
        P("ctx", None),
        P(("ctx", "exp"), None),
        P(("ctx", "exp")),
        P(("ctx", "exp"), None),
        P(("ctx", "exp"), None, None),
        P(("ctx", "exp"), None),
        P(("ctx", "exp"), None),
    )
    out_specs = (
        P(("ctx", "exp"), None),
        P("ctx", "exp"),
        P("ctx", "exp"),
        P("ctx", "exp", None, None, None),
        P(("ctx", "exp"), None),
    )
    return jax.shard_map(local, mesh=mesh, in_specs=in_specs, out_specs=out_specs, check_vma=False)
```
